32 devices in a mesh: seg: 16 (over z, y, x), dir: 2 (over core).
Axes of the slice: x: 2, y: 2, z: 4, core: 2. Of those that a mesh axis runs over, the one named last changes fastest.
Arguments:
- strain: float32 [128, 8, 6, 8192], P('seg'), may hold values from -6 to 6
- valid_flags: int32 [128, 8], P('seg'), may hold values from 0 to 1, as said below
- direction_ids: int32 [1024], P('dir'), may hold values from 0 to 3071
- grid_patterns: float32 [3072, 6], replicated, may hold values from -1 to 1
- grid_delays: float32 [3072, 3], replicated, may hold values from -40 to 40
Outputs:
- peak: float32 [8, 8192], P(None, 'seg')
- dir_score: float32 [8, 1024], P(None, 'dir')
The draws below stay inside these ranges and needn't reach their ends.
Inputs may be any that keep to these rules, and one draw needn't show every extreme that they name: `valid_flags`: in every draw one window has no usable segment.
All inputs are finite; a program needn't handle non-finite values.
Results may differ from the reference program's by a relative error of at most 0.0001.
Values sent between devices are 32-bit elements; how exact they have to be, the bound alone decides.
No kernel may reach another device: no remote copies, remote signals or barrier semaphores. Data moves between devices by JAX's collectives and lax.ppermute only.
A program may use at most 64 MiB of HBM per device.

```python
import math
import jax
import jax.numpy as jnp
from jax import lax

F = 8192
K = 1024
GRID = 3072
WIN = 8
SEGS = 128


def draw_valid_flags(key, part):
    key_levels, key_window = jax.random.split(jax.random.fold_in(key, 7331))
    levels = jax.random.randint(key_levels, (SEGS, WIN), 0, 4 * SEGS)
    position = jnp.arange(SEGS, dtype=jnp.int32)[:, None]
    usable = (levels < SEGS + 3 * position).astype(jnp.int32)
    silent_window = jax.random.randint(key_window, (), 0, WIN)
    keeper = (jnp.arange(WIN, dtype=jnp.int32)[None, :] != silent_window).astype(jnp.int32)
    return usable * keeper


def place_ends(array, rng, smallest, largest):
    spot = [jax.random.randint(jax.random.fold_in(rng, axis), (), 0, length) for axis, length in enumerate(array.shape)]
    longest = array.shape.index(max(array.shape))
    next_to = spot[:longest] + [(spot[longest] + 1) % array.shape[longest]] + spot[longest + 1:]
    return array.at[tuple(spot)].set(smallest).at[tuple(next_to)].set(largest)


def with_spikes(entries, stream_key, source, target, blocks, factor):
    owner, partner = [(jnp.arange(entries.shape[dim]) // (entries.shape[dim] // blocks)).reshape([-1 if axis == dim else 1 for axis in range(entries.ndim)]) for dim in (source, target)]
    chosen = jax.random.permutation(stream_key, blocks)[partner]
    strong = (owner == chosen) | (owner == (partner + blocks // 2) % blocks)
    return jnp.where(strong, factor * entries, entries)


def shard_levels(own_key, shape, pieces, smallest, top_value):
    def one(dim, blocks):
        draws = jax.random.uniform(jax.random.fold_in(jax.random.fold_in(own_key, 6), dim), (blocks,), jnp.float32, smallest / len(pieces), top_value / len(pieces))
        return jnp.repeat(jnp.exp(draws), shape[dim] // blocks).reshape((-1,) + (1,) * (len(shape) - dim - 1))

    loudness = one(*pieces[0])
    for cut in pieces[1:]:
        loudness = loudness * one(*cut)
    return loudness


def noise_with(own_key, shape, deviation, most, shards, heavy, held_as=jnp.bfloat16):
    entries = deviation * jax.random.normal(own_key, shape, jnp.float32)
    if shards:
        entries = entries * shard_levels(own_key, shape, shards, -0.22, 0.18)
    return jnp.clip(with_spikes(entries, jax.random.fold_in(own_key, 3), *heavy), -most, most).astype(held_as)


def setup_inputs(seed: int = 0) -> dict:
    seeds = jax.random.split(jax.random.key(seed), 6)
    strain = noise_with(seeds[0], (SEGS, WIN, 6, F), 1.0, 6.0, ((0, 16),), (0, 3, 16, 2.0), jnp.float32)
    valid_flags = draw_valid_flags(jax.random.fold_in(seeds[5], 71), 0)
    direction_ids = place_ends(jax.random.randint(seeds[2], (K,), 0, GRID), jax.random.fold_in(seeds[2], 1), 0, GRID - 1).astype(jnp.int32)
    grid_patterns = jnp.clip(jax.random.uniform(seeds[3], (GRID, 6), jnp.float32, -1.0, 1.0), -1.0, 1.0)
    grid_delays = jnp.clip(jax.random.uniform(seeds[4], (GRID, 3), jnp.float32, -40.0, 40.0), -40.0, 40.0)
    return dict(strain=strain, valid_flags=valid_flags, direction_ids=direction_ids, grid_patterns=grid_patterns, grid_delays=grid_delays)


PAIRS = ((0, 1), (0, 2), (1, 2))


def spectra(strain, valid_flags):
    weight = valid_flags.astype(jnp.float32)[:, :, None]
    real_part = strain[:, :, 0:3, :]
    imag_part = strain[:, :, 3:6, :]
    parts = []
    for d in range(3):
        parts.append(jnp.sum(weight * (real_part[:, :, d] * real_part[:, :, d] + imag_part[:, :, d] * imag_part[:, :, d]), 0))
    for d, e in PAIRS:
        parts.append(jnp.sum(weight * (real_part[:, :, d] * real_part[:, :, e] + imag_part[:, :, d] * imag_part[:, :, e]), 0))
    for d, e in PAIRS:
        parts.append(jnp.sum(weight * (imag_part[:, :, d] * real_part[:, :, e] - real_part[:, :, d] * imag_part[:, :, e]), 0))
    return jnp.stack(parts, 0)


def null_vectors(rows):
    plus = rows[:, 0:3]
    cross = rows[:, 3:6]
    first = plus[:, 1] * cross[:, 2] - plus[:, 2] * cross[:, 1]
    second = plus[:, 2] * cross[:, 0] - plus[:, 0] * cross[:, 2]
    third = plus[:, 0] * cross[:, 1] - plus[:, 1] * cross[:, 0]
    null = jnp.stack([first, second, third], 1)
    norm2 = jnp.maximum(jnp.sum(null * null, 1), 0.25)
    return null, norm2


def project(cov, first_bin, null, norm2, delays, count, total_bins):
    width = cov.shape[2]
    freq = (first_bin + jnp.arange(width, dtype=jnp.int32)).astype(jnp.float32) * (2.0 * math.pi / total_bins)
    energy = jnp.zeros((null.shape[0], cov.shape[1], width), jnp.float32)
    for d in range(3):
        energy = energy + (null[:, d] * null[:, d])[:, None, None] * cov[d][None]
    for index, (d, e) in enumerate(PAIRS):
        angle = (delays[:, d] - delays[:, e])[:, None] * freq[None, :]
        factor = (2.0 * null[:, d] * null[:, e])[:, None, None]
        energy = energy + factor * (jnp.cos(angle)[:, None, :] * cov[3 + index][None] + jnp.sin(angle)[:, None, :] * cov[6 + index][None])
    return energy / (norm2[:, None, None] * jnp.maximum(count, 1.0)[None, :, None])


def reference(strain, valid_flags, direction_ids, grid_patterns, grid_delays):
    cov = spectra(strain, valid_flags)
    count = jnp.sum(valid_flags.astype(jnp.float32), 0)
    rows = grid_patterns[direction_ids]
    delays = grid_delays[direction_ids]
    null, norm2 = null_vectors(rows)
    block = math.gcd(K, 64)
    blocks = K // block

    def one_block(items):
        power = project(cov, 0, items[0], items[1], items[2], count, F)
        return jnp.max(power, 0), jnp.sum(power, 2) / F

    peaks, scores = lax.map(one_block, (null.reshape(blocks, block, 3), norm2.reshape(blocks, block), delays.reshape(blocks, block, 3)))
    peak = jnp.max(peaks, 0)
    dir_score = scores.reshape(K, WIN).T
    return peak, dir_score
```

```python
import math

import jax
import jax.numpy as jnp
from jax import lax
from jax.experimental import pallas as pl
from jax.experimental.pallas import tpu as pltpu
from jax.sharding import PartitionSpec as P

LANES = 128
FAN = 4
MIB = 1 << 20


def sincos(x):
    turns = jnp.floor(x * (2.0 / math.pi) + 0.5)
    r = x - turns * 1.5703125
    r = r - turns * 4.837512969970703125e-4
    r = r - turns * 7.54978995489188216e-8
    z = r * r
    s = r + r * z * (-1.6666654611e-1 + z * (8.3321608736e-3 + z * (-1.9515295891e-4)))
    c = 1.0 - 0.5 * z + z * z * (4.166664568298827e-2 + z * (-1.388731625493765e-3 + z * 2.443315711809948e-5))
    q = turns.astype(jnp.int32)
    swap = (q & 1) == 1
    sin = jnp.where(swap, c, s)
    cos = jnp.where(swap, s, c)
    sin = jnp.where((q & 2) == 2, -sin, sin)
    cos = jnp.where(((q + 1) & 2) == 2, -cos, cos)
    return sin, cos


def times(a, b):
    return a[0] * b[0] - a[1] * b[1], a[1] * b[0] + a[0] * b[1]


def hi_lo(x):
    hi = x.astype(jnp.bfloat16)
    return hi, (x - hi.astype(jnp.float32)).astype(jnp.bfloat16)


def direction_rows(ids_refs, patterns, delays, grid_points):
    picked = []
    for ref in ids_refs:
        for row in range(ref.shape[0]):
            ids = ref[row : row + 1, :]
            page = jnp.broadcast_to(ids >> 7, (8, LANES))
            lane = jnp.broadcast_to(ids & 127, (8, LANES))
            first = jnp.zeros((8, LANES), jnp.float32)
            second = first
            for h in range(grid_points // LANES):
                here = page == h
                cut = slice(h * LANES, (h + 1) * LANES)
                first = jnp.where(here, jnp.take_along_axis(patterns[:, cut], lane, axis=1), first)
                second = jnp.where(here, jnp.take_along_axis(delays[:, cut], lane, axis=1), second)
            picked.append((first, second))
    first = jnp.concatenate([a for a, _ in picked], 1)
    second = jnp.concatenate([b for _, b in picked], 1)
    plus = [first[d : d + 1] for d in range(3)]
    cross = [first[d : d + 1] for d in range(3, 6)]
    null = [
        plus[1] * cross[2] - plus[2] * cross[1],
        plus[2] * cross[0] - plus[0] * cross[2],
        plus[0] * cross[1] - plus[1] * cross[0],
    ]
    norm2 = jnp.maximum(null[0] * null[0] + null[1] * null[1] + null[2] * null[2], 0.25)
    lag = [second[0:1] - second[1:2], second[1:2] - second[2:3]]
    squares = [n * n / norm2 for n in null]
    pairs = [2.0 * null[0] * null[1] / norm2, 2.0 * null[0] * null[2] / norm2, 2.0 * null[1] * null[2] / norm2]
    return lag, pairs, squares


def front_kernel(cfg, strain, flags, ids_a, ids_b, grid_patterns, grid_delays, *rest):
    n, share, width, ndir, bins = cfg["n"], cfg["share"], cfg["width"], cfg["ndir"], cfg["bins"]
    outs, rows_out = rest[:FAN], rest[FAN]
    tables, held, patterns, delays, sems, table_sem = rest[FAN + 1 :]
    segs = strain.shape[0]
    me = lax.axis_index("seg")
    base = lax.axis_index("dir") * width if cfg["split"] > 1 else 0
    blocks = n // FAN

    copies = [
        pltpu.make_async_copy(grid_patterns, patterns.at[0:6], table_sem.at[0]),
        pltpu.make_async_copy(grid_delays, delays.at[0:3], table_sem.at[1]),
    ]
    for copy in copies:
        copy.start()
    reads = []
    for t in range(n):
        start = pl.multiple_of((me ^ t) * share + base, LANES)
        reads.append(pltpu.make_async_copy(strain.at[:, :, :, pl.ds(start, width)], held.at[t], sems.at[t]))
        reads[-1].start()
    for copy in copies:
        copy.wait()

    ids = [ids_a] if ids_b is None else [ids_a, ids_b]
    lag, pairs, squares = direction_rows(ids, patterns, delays, grid_patterns.shape[1])
    turn = 2.0 * math.pi / bins
    rows_out[...] = jnp.concatenate([lag[0], lag[1], *pairs, *squares], 0)

    low = lax.broadcasted_iota(jnp.int32, (8, ndir), 0).astype(jnp.float32) * turn
    grown = []
    for p in range(2):
        s, c = sincos(lag[p] * low)
        c_all, s_all = c, s
        size = 8
        while size < width:
            sj, cj = sincos(lag[p] * (size * turn))
            cn, sn = times((c_all, s_all), (cj, sj))
            c_all, s_all = jnp.concatenate([c_all, cn], 0), jnp.concatenate([s_all, sn], 0)
            size *= 2
        grown.append((c_all, s_all))
    at = [grown[0], times(grown[0], grown[1]), grown[1]]
    for p in range(3):
        for half in range(2):
            hi, lo = hi_lo(at[p][half])
            tables[p, 0, half * width : (half + 1) * width] = hi
            tables[p, 1, half * width : (half + 1) * width] = lo

    first_bin = ((lax.broadcasted_iota(jnp.int32, (n, ndir), 0) ^ me) * share + base).astype(jnp.float32) * turn
    far = []
    for p in range(2):
        s, c = sincos(lag[p] * first_bin)
        far.append((c, s))
    far = [far[0], times(far[0], far[1]), far[1]]

    weight = flags[...].astype(jnp.float32)
    masks = [jnp.broadcast_to(weight[:, s : s + 1], (8, width)) for s in range(segs)]
    totals = [jnp.zeros((8, width), jnp.float32) for _ in range(3)]
    for t in range(n):
        reads[t].wait()
        out, q = outs[t % FAN], (t // FAN) * 9
        acc = [jnp.zeros((8, width), jnp.float32) for _ in range(9)]
        for s in range(segs):
            x = [held[t, s, c] for c in range(6)]
            y = [masks[s] * v for v in x]
            for d in range(3):
                acc[d] = acc[d] + (y[d] * x[d] + y[d + 3] * x[d + 3])
            for i, (d, e) in enumerate(((0, 1), (0, 2), (1, 2))):
                acc[3 + i] = acc[3 + i] + (y[d] * x[e] + y[d + 3] * x[e + 3])
                acc[6 + i] = acc[6 + i] + (y[d + 3] * x[e] - y[d] * x[e + 3])
        for c in range(9):
            out[q + c] = acc[c]
        for d in range(3):
            totals[d] = totals[d] + acc[d]

    score = jnp.zeros((8, ndir), jnp.float32)
    for d in range(3):
        score = score + jnp.sum(totals[d], 1, keepdims=True) * squares[d]
    for p in range(3):
        real = jnp.concatenate([outs[t % FAN][(t // FAN) * 9 + 3 + p] for t in range(n)], 0)
        imag = jnp.concatenate([outs[t % FAN][(t // FAN) * 9 + 6 + p] for t in range(n)], 0)
        left = jnp.concatenate([jnp.concatenate([real, imag], 1), jnp.concatenate([imag, -real], 1)], 0)
        hi, lo = hi_lo(left)
        dot = lambda a, b: jnp.dot(a, b, preferred_element_type=jnp.float32)
        both = dot(hi, tables[p, 0]) + dot(lo, tables[p, 0]) + dot(hi, tables[p, 1])
        part = jnp.zeros((8, ndir), jnp.float32)
        for t in range(n):
            part = part + far[p][0][t : t + 1] * both[t * 8 : t * 8 + 8]
            part = part + far[p][1][t : t + 1] * both[(n + t) * 8 : (n + t) * 8 + 8]
        score = score + pairs[p] * part
    score = score * (1.0 / bins)
    count = jnp.broadcast_to(jnp.sum(weight, 1, keepdims=True), (8, width))
    for out in outs:
        for i in range(ndir // width):
            out[blocks * 9 + i] = score[:, i * width : (i + 1) * width]
        out[blocks * 9 + ndir // width] = count


def merge_kernel(blocks, extra, *refs):
    ins, outs = refs[:FAN], refs[FAN:]
    add = lambda i: (ins[0][i] + ins[1][i]) + (ins[2][i] + ins[3][i])
    for b in range(blocks):
        for c in range(9):
            outs[b % FAN][(b // FAN) * 9 + c] = add(b * 9 + c)
    for i in range(extra):
        tail = add(blocks * 9 + i)
        for out in outs:
            out[(blocks // FAN) * 9 + i] = tail


def factor_kernel(cfg, rows, *outs):
    share, width, ndir, bins = cfg["share"], cfg["width"], cfg["ndir"], cfg["bins"]
    factors, squares = outs
    first = lax.axis_index("seg") * share + (lax.axis_index("dir") * width if cfg["split"] > 1 else 0)
    freq = (lax.broadcasted_iota(jnp.int32, (1, width), 1) + first).astype(jnp.float32) * (2.0 * math.pi / bins)
    step = LANES
    for k in range(0, ndir, step):
        cols = jnp.transpose(rows[:, k : k + step], (1, 0))
        col = lambda i, w: jnp.broadcast_to(cols[:, i : i + 1], (step, w))
        here = []
        for p in range(2):
            s, c = sincos(col(p, width) * freq)
            here.append((c, s))
        here = [here[0], times(here[0], here[1]), here[1]]
        for p in range(3):
            scale = col(2 + p, width)
            factors[p, k : k + step] = scale * here[p][0]
            factors[3 + p, k : k + step] = scale * here[p][1]
        for d in range(3):
            squares[d, k : k + step] = col(5 + d, LANES)


def project_kernel(cfg, *refs):
    width, ndir = cfg["width"], cfg["ndir"]
    ins, (factors, squares), (keep, send), (spread,) = refs[:FAN], refs[FAN : FAN + 2], refs[FAN + 2 : FAN + 4], refs[FAN + 4 :]
    add = lambda i: (ins[0][i] + ins[1][i]) + (ins[2][i] + ins[3][i])
    scale = 1.0 / jnp.maximum(add(9 + ndir // width), 1.0)
    step = 16
    for f in range(0, width, LANES):
        lanes = slice(f, f + LANES)
        for c in range(9):
            cov = add(c)[:, lanes]
            for w in range(8):
                spread[c, w] = jnp.broadcast_to(cov[w : w + 1], (8, LANES))

        def body(i, best):
            k = pl.multiple_of(i * step, step)
            best = list(best)
            for j in range(0, step, 8):
                a = [squares[d, pl.ds(k + j, 8)] for d in range(3)]
                a += [factors[c, pl.ds(k + j, 8), lanes] for c in range(6)]
                for w in range(8):
                    terms = [a[c] * spread[c, w] for c in range(9)]
                    while len(terms) > 1:
                        terms = [terms[m] + terms[m + 1] if m + 1 < len(terms) else terms[m] for m in range(0, len(terms), 2)]
                    best[w] = jnp.maximum(best[w], terms[0])
            return tuple(best)

        low = jnp.full((8, LANES), -jnp.inf, jnp.float32)
        best = lax.fori_loop(0, ndir // step, body, (low,) * 8)
        peak = jnp.concatenate([jnp.max(b, 0, keepdims=True) for b in best], 0) * scale[:, lanes]
        keep[:, lanes] = peak
        send[:, lanes] = peak
    half = ndir // width // cfg["split"]
    for i in range(half):
        keep[:, (1 + i) * width : (2 + i) * width] = add(9 + i) * scale
        if cfg["split"] > 1:
            send[:, (1 + i) * width : (2 + i) * width] = add(9 + half + i) * scale


def finish_kernel(cfg, keep, other, peak, score):
    width, split = cfg["width"], cfg["split"]
    if split > 1:
        core = lax.axis_index("dir")
        peak[:, pl.ds(pl.multiple_of(core * width, LANES), width)] = keep[:, :width]
        peak[:, pl.ds(pl.multiple_of((1 - core) * width, LANES), width)] = other[:, :width]
        score[...] = keep[:, width:] + other[:, width:]
    else:
        peak[...] = jnp.maximum(keep[:, :width], other[:, :width])
        score[...] = keep[:, width:]


def call(kernel, out_shape, in_spaces, vmem, scratch=(), flops=0, nbytes=0, name=None):
    spec = {"v": pltpu.VMEM, "a": pl.ANY}
    return pl.pallas_call(
        kernel,
        out_shape=out_shape,
        in_specs=[pl.BlockSpec(memory_space=spec[s]) for s in in_spaces],
        out_specs=jax.tree.map(lambda _: pl.BlockSpec(memory_space=pltpu.VMEM), out_shape),
        scratch_shapes=scratch,
        compiler_params=pltpu.CompilerParams(vmem_limit_bytes=vmem * MIB),
        cost_estimate=pl.CostEstimate(flops=flops, bytes_accessed=nbytes, transcendentals=0),
        name=name,
    )


def shards(strain, valid_flags, direction_ids, grid_patterns, grid_delays):
    n, pair = lax.axis_size("seg"), lax.axis_size("dir")
    segs, windows, _, bins = strain.shape
    grid_points = grid_patterns.shape[0]
    share = bins // n
    split = pair if share % (pair * LANES) == 0 else 1
    width = share // split
    own = direction_ids.shape[0]
    ndir = own * split
    cfg = dict(n=n, share=share, split=split, width=width, ndir=ndir, bins=bins)
    f32 = lambda *shape: jax.ShapeDtypeStruct(shape, jnp.float32)
    swap = [(i, i ^ 1) for i in range(pair)]

    ids = direction_ids.reshape(own // LANES, LANES)
    lists = [ids] + ([lax.ppermute(ids, "dir", swap)] if split > 1 else [])
    extra = ndir // width + 1
    blocks = n // FAN

    def front(*refs):
        if split > 1:
            front_kernel(cfg, *refs)
        else:
            front_kernel(cfg, *refs[:3], None, *refs[3:])

    *parts, rows = call(
        front,
        [f32(blocks * 9 + extra, 8, width)] * FAN + [f32(8, ndir)],
        "av" + "v" * len(lists) + "aa",
        40,
        [
            pltpu.VMEM((3, 2, 2 * width, ndir), jnp.bfloat16),
            pltpu.VMEM((n, segs, 6, windows, width), jnp.float32),
            pltpu.VMEM((8, grid_points), jnp.float32),
            pltpu.VMEM((8, grid_points), jnp.float32),
            pltpu.SemaphoreType.DMA((n,)),
            pltpu.SemaphoreType.DMA((2,)),
        ],
        name="front",
    )(jnp.transpose(strain, (0, 2, 1, 3)), valid_flags.T, *lists, grid_patterns.T, grid_delays.T)

    factors, squares = call(
        lambda *refs: factor_kernel(cfg, *refs),
        [f32(6, ndir, width), f32(3, ndir, LANES)],
        "v",
        20,
        flops=ndir * width * 60,
        nbytes=ndir * width * 24,
        name="factors",
    )(rows)

    offset = 1
    while True:
        seen = [parts[0]]
        for r in range(1, FAN):
            seen.append(lax.ppermute(parts[r], "seg", [(i, i ^ (r * offset)) for i in range(n)]))
        offset *= FAN
        if blocks == 1:
            break
        parts = call(
            lambda *refs: merge_kernel(blocks, extra, *refs),
            [f32(blocks // FAN * 9 + extra, 8, width)] * FAN,
            "vvvv",
            8,
            name="merge",
        )(*seen)
        blocks //= FAN

    keep, send = call(
        lambda *refs: project_kernel(cfg, *refs),
        [f32(8, width + own), f32(8, width + own if split > 1 else width)],
        "vvvvvv",
        20,
        [pltpu.VMEM((9, 8, 8, LANES), jnp.float32)],
        name="project",
    )(*seen, factors, squares)
    other = lax.ppermute(send, "dir", swap)
    return tuple(
        call(
            lambda *refs: finish_kernel(cfg, *refs),
            [f32(8, share), f32(8, own)],
            "vv",
            2,
            name="finish",
        )(keep, other)
    )


def solution(mesh):
    placed = (P("seg", None, None, None), P("seg", None), P("dir"), P(), P())
    return jax.shard_map(
        shards,
        mesh=mesh,
        in_specs=placed,
        out_specs=(P(None, "seg"), P(None, "dir")),
        check_vma=False,
    )
```
